128 devices in a mesh: ax: 8 (over x_hi, z), az: 16 (over y, x_lo, core).
Axes of the slice: x: 4 (x_hi: 2, x_lo: 2; x = x_hi * 2 + x_lo), y: 4, z: 4, core: 2. Of those that a mesh axis runs over, the one named last changes fastest.
Arguments:
- adjoint: float32 [3, 256, 1024, 256], P(None, 'ax', 'az'), may hold values from -6 to 6
- primal: float32 [3, 256, 1024, 256], P(None, 'ax', 'az'), may hold values from -6 to 6
- wall: int32 [256, 1024], P('ax', 'az'), may hold values from 0 to 63
- owner: int32 [256, 1024], P('ax', 'az'), may hold values from 0 to 4095, as said below
- adjacency: int32 [8, 512, 4], P('ax', 'az'), may hold values from 0 to 95
- counts: int32 [8, 512], P('ax', 'az'), may hold values from 32 to 128
- laplacian: float32 [8, 512, 128, 128], P('ax', 'az'), as said below
Outputs:
- adjoint_next: float32 [3, 256, 1024, 256], P(None, 'ax', 'az')
- smoothed: float32 [8, 512, 128], P('ax', 'az')
The draws below stay inside these ranges and needn't reach their ends.
Inputs may be any that keep to these rules, and one draw needn't show every extreme that they name: `owner`: patch p lives on device p // 32 of the mesh in order ax then az. Among the columns of one device, at most 48 have owners on one device, and in every draw some owning devices receive exactly 48 from every device. `laplacian`: diagonal entries lie in 2 to 3, off-diagonal ones in -2 / 128 to 0.
All inputs are finite; a program needn't handle non-finite values.
Results may differ from the reference program's by a relative error of at most 0.0001.
Values sent between devices are 32-bit elements; how exact they have to be, the bound alone decides.
No kernel may reach another device: no remote copies, remote signals or barrier semaphores. Data moves between devices by JAX's collectives and lax.ppermute only.
A program may use at most 128 MiB of HBM per device.

```python
import jax
import jax.numpy as jnp
from jax import lax

CX = 32
CA = 64
CR = 256
PV = 128
NP_DEV = 32
NEIGH = 4
SWEEPS = 3
NXG = 256
NAG = 1024
PATCH_AZ = 512
N_AX = 8
N_AZ = 16


def draw_owner(key, part):
    devices_all = N_AX * N_AZ
    tiles_dev = CX * CA
    capacity = 3 * tiles_dev // devices_all
    slots_all = devices_all * capacity
    ranking = jax.random.permutation(jax.random.fold_in(key, 1), devices_all)
    heated = (ranking < devices_all // 4).astype(jnp.int32)

    def per_source(source_index):
        subkey = jax.random.fold_in(jax.random.fold_in(key, 7), source_index)
        slot_ids = jnp.arange(slots_all, dtype=jnp.int32)
        noise = jax.random.randint(jax.random.fold_in(subkey, 0), (slots_all,), 0, 4096)
        scores = (noise + heated[slot_ids // capacity] * 8192) * slots_all + slot_ids
        picked = lax.top_k(scores, tiles_dev)[1].astype(jnp.int32)
        target = picked // capacity
        shuffle = jax.random.permutation(jax.random.fold_in(subkey, 1), tiles_dev)
        target = target[shuffle]
        within = jax.random.randint(jax.random.fold_in(subkey, 2), (tiles_dev,), 0, NP_DEV)
        return target * NP_DEV + within
    owners = jax.vmap(per_source)(jnp.arange(devices_all, dtype=jnp.int32))
    owners = owners.reshape(N_AX, N_AZ, CX, CA).transpose(0, 2, 1, 3)
    return owners.reshape(N_AX * CX, N_AZ * CA).astype(jnp.int32)


def draw_laplacian(key, part):
    shape = (N_AX, NP_DEV * N_AZ, PV, PV)
    offdiag = -jax.random.uniform(jax.random.fold_in(key, 1), shape, jnp.float32, 0.0, 2.0 / PV)
    diagonal = 2.0 + jax.random.uniform(jax.random.fold_in(key, 2), shape[:3], jnp.float32)
    row_ids = lax.broadcasted_iota(jnp.int32, shape, 2)
    col_ids = lax.broadcasted_iota(jnp.int32, shape, 3)
    return jnp.where(row_ids == col_ids, diagonal[..., None], offdiag).astype(jnp.float32)


def with_ends(result, key, least, largest):
    index_at = [jax.random.randint(jax.random.fold_in(key, axis), (), 0, length) for axis, length in enumerate(result.shape)]
    longest = result.shape.index(max(result.shape))
    neighbour = index_at[:longest] + [(index_at[longest] + 1) % result.shape[longest]] + index_at[longest + 1:]
    return result.at[tuple(index_at)].set(least).at[tuple(neighbour)].set(largest)


def block_scale(rng, shape, split, least, largest):
    def one(position, parts):
        heights = jax.random.uniform(jax.random.fold_in(jax.random.fold_in(rng, 6), position), (parts,), jnp.float32, least / len(split), largest / len(split))
        return jnp.repeat(jnp.exp(heights), shape[position] // parts).reshape((-1,) + (1,) * (len(shape) - position - 1))

    loudness = one(*split[0])
    for cut in split[1:]:
        loudness = loudness * one(*cut)
    return loudness


def bell_draw(stream_key, shape, spread, reach, shards=(), kind=jnp.bfloat16):
    drawn = jax.random.normal(stream_key, shape, jnp.float32) * spread
    if len(shards) > 0:
        drawn = block_scale(stream_key, shape, shards, -0.22, 0.18) * drawn
    return jnp.clip(drawn, min=-reach, max=reach).astype(kind)


def setup_inputs(seed: int = 0) -> dict:
    streams_of = jax.random.split(jax.random.key(seed), 8)
    adjoint = bell_draw(streams_of[0], (3, NXG, NAG, CR), 1.0, 6.0, ((1, 8), (2, 16)), jnp.float32)
    primal = bell_draw(streams_of[1], (3, NXG, NAG, CR), 1.0, 6.0, ((1, 8), (2, 16)), jnp.float32)
    wall = with_ends(jax.random.randint(streams_of[2], (NXG, NAG), 0, CR // 4), jax.random.fold_in(streams_of[2], 1), 0, (CR // 4) - 1).astype(jnp.int32)
    owner = draw_owner(jax.random.fold_in(streams_of[7], 71), 0)
    adjacency = with_ends(jax.random.randint(streams_of[4], (N_AX, PATCH_AZ, NEIGH), 0, 3 * NP_DEV), jax.random.fold_in(streams_of[4], 1), 0, (3 * NP_DEV) - 1).astype(jnp.int32)
    counts = with_ends(jax.random.randint(streams_of[5], (N_AX, PATCH_AZ), PV // 4, PV + 1), jax.random.fold_in(streams_of[5], 1), PV // 4, PV).astype(jnp.int32)
    laplacian = draw_laplacian(jax.random.fold_in(streams_of[7], 71), 0)
    return {"adjoint": adjoint, "primal": primal, "wall": wall, "owner": owner, "adjacency": adjacency, "counts": counts, "laplacian": laplacian}


time_step = 0.12
viscosity = 1.0
wall_scale = 0.1
smoothing = 0.5
coupling = 0.25
relaxation = 0.25


def adjoint_update(masked, primal, fluid, x_plus, x_minus, a_plus, a_minus):
    radial = jnp.pad(masked, ((0, 0), (0, 0), (0, 0), (1, 1)))
    r_plus = radial[..., 2:]
    r_minus = radial[..., :-2]
    laplace = x_plus + x_minus + a_plus + a_minus + r_plus + r_minus - 6.0 * masked
    advect = primal[0][None] * (x_plus - x_minus) * 0.5
    advect = advect + primal[1][None] * (a_plus - a_minus) * 0.5
    advect = advect + primal[2][None] * (r_plus - r_minus) * 0.5
    return fluid[None] * (masked + time_step * (viscosity * laplace + advect))


def take_rows(field, index):
    return field[index]


def reference(adjoint, primal, wall, owner, adjacency, counts, laplacian):
    depth = lax.broadcasted_iota(jnp.int32, wall.shape + (CR,), 2)
    fluid = (depth >= wall[:, :, None]).astype(jnp.float32)
    masked = adjoint * fluid[None]
    padded = jnp.pad(masked, ((0, 0), (1, 1), (0, 0), (0, 0)))
    updated = adjoint_update(masked, primal, fluid, padded[:, 2:], padded[:, :-2],
                             jnp.roll(masked, -1, axis=2), jnp.roll(masked, 1, axis=2))
    tiles = jnp.sum(primal[..., :PV] * updated[..., :PV], axis=0)
    source = jax.ops.segment_sum(tiles.reshape(-1, PV), owner.reshape(-1),
                                 num_segments=N_AX * PATCH_AZ) * wall_scale
    source = source.reshape(N_AX, PATCH_AZ, PV)
    vertex = lax.broadcasted_iota(jnp.int32, (N_AX, PATCH_AZ, PV), 2)
    live = (vertex < counts[:, :, None]).astype(jnp.float32)
    rows = lax.broadcasted_iota(jnp.int32, adjacency.shape, 1)
    source_rows = ((rows // NP_DEV) * NP_DEV - NP_DEV + adjacency) % PATCH_AZ
    field = live * source
    for sweep in range(SWEEPS):
        gathered = jax.vmap(take_rows)(field, source_rows)
        neighbours = jnp.sum(gathered, axis=2)
        applied = jnp.einsum("ipvw,ipw->ipv", laplacian, field, precision=lax.Precision.HIGHEST)
        image = field + smoothing * (applied + coupling * (NEIGH * field - neighbours))
        field = live * (field + relaxation * (source - image))
    return updated, field
```

```python
import jax
import jax.numpy as jnp
import numpy as np
from jax import lax
from jax.experimental import pallas as pl
from jax.experimental.pallas import tpu as pltpu
from jax.sharding import Mesh, PartitionSpec as P

SWEEPS = 3
time_step = 0.12
viscosity = 1.0
wall_scale = 0.1
smoothing = 0.5
coupling = 0.25
relaxation = 0.25

CHIP = ("xh", "z", "y", "xl")
AX = ("xh", "z")
AZ = ("y", "xl", "c")
BANKS = 4
XB = 4


def pairs_a(n):
    return [(i, i ^ 1) for i in range(n)]


def pairs_b(n):
    return [(i, (i + 1) % n if i % 2 else (i - 1) % n) for i in range(n)]


def pairs_q(n):
    return [p for i in range(1, n - 1, 2) for p in ((i, i + 1), (i + 1, i))]


def grid_kernel(flags, rows, adj, prim, fluid, xp_in, xq_in, aa_in, ab_in,
                upd, keep, send,
                mlo, mhi, plo, phi, olo, ohi, tiles, bank0, bank1, bank2, bank3,
                sem_in, sem_x, sem_out):
    banks = (bank0, bank1, bank2, bank3)
    nx = adj.shape[1]
    na = adj.shape[2]
    nb = nx // XB
    core = flags[0]
    odd = flags[1]

    def loads(k):
        xs = pl.ds(k * XB, XB)
        xd = pl.ds(1 + k * XB, XB)
        return (
            pltpu.make_async_copy(adj.at[:, xs, :, 0:128], mlo.at[:, xd, 8:8 + na, :], sem_in.at[k, 0]),
            pltpu.make_async_copy(adj.at[:, xs, :, 128:256], mhi.at[:, xd, 8:8 + na, :], sem_in.at[k, 1]),
            pltpu.make_async_copy(prim.at[:, xs, :, 0:128], plo.at[:, xs], sem_in.at[k, 2]),
            pltpu.make_async_copy(prim.at[:, xs, :, 128:256], phi.at[:, xs], sem_in.at[k, 3]),
        )

    plane_p = jnp.where(odd == 0, nx + 1, 0)
    plane_q = jnp.where(odd == 0, 0, nx + 1)
    halos = []
    for n, (src, plane) in enumerate(((xp_in, plane_p), (xq_in, plane_q))):
        for h, dst in enumerate((mlo, mhi)):
            halos.append(pltpu.make_async_copy(
                src.at[:, :, 128 * h:128 * h + 128], dst.at[:, plane, 8:8 + na, :], sem_x.at[n, h]))

    def start(k, _):
        for cp in loads(k):
            cp.start()
        return 0

    lax.fori_loop(0, 1, start, 0)
    for cp in halos:
        cp.start()
    lax.fori_loop(1, nb, start, 0)

    zero8 = jnp.zeros((64, 128), jnp.float32)

    def clear(i, _):
        for b in banks:
            b[pl.ds(i * 64, 64), :] = zero8
        return 0

    lax.fori_loop(0, bank0.shape[0] // 64, clear, 0)

    row_a = jnp.where(core == 0, 8 + na, 7)
    row_b = jnp.where(core == 0, 7, 8 + na)

    def edges(x, _):
        for src, row in ((aa_in, row_a), (ab_in, row_b)):
            for c in range(3):
                mlo[c, 1 + x, pl.ds(row, 1), :] = src[0, c, pl.ds(x, 1), :]
                mhi[c, 1 + x, pl.ds(row, 1), :] = src[1, c, pl.ds(x, 1), :]
        return 0

    def mask(x):
        for a in range(0, na, 16):
            f = fluid[x, a:a + 16, :]
            for c in range(3):
                mlo[c, 1 + x, 8 + a:24 + a, :] = mlo[c, 1 + x, 8 + a:24 + a, :] * f

    alpha = time_step * viscosity
    half = 0.5 * time_step
    lane = lax.broadcasted_iota(jnp.int32, (16, 128), 1)

    def column(x, low):
        m, other, p, o = (mlo, mhi, plo, olo) if low else (mhi, mlo, phi, ohi)
        for a in range(0, na, 16):
            pv = [p[c, x, a:a + 16, :] for c in range(3)]
            q = [half * v for v in pv]
            up = [alpha + v for v in q]
            dn = [alpha - v for v in q]
            if low:
                dn[2] = jnp.where(lane == 0, 0.0, dn[2])
                f = fluid[x, a:a + 16, :]
                t = None
            else:
                up[2] = jnp.where(lane == 127, 0.0, up[2])
            for c in range(3):
                mid = m[c, 1 + x, 8 + a:24 + a, :]
                oth = other[c, 1 + x, 8 + a:24 + a, :]
                rp = pltpu.roll(mid, 127, 1)
                rm = pltpu.roll(mid, 1, 1)
                if low:
                    rp = jnp.where(lane == 127, pltpu.roll(oth, 127, 1), rp)
                else:
                    rm = jnp.where(lane == 0, pltpu.roll(oth, 1, 1), rm)
                s = mid * (1.0 - 6.0 * alpha)
                s = s + m[c, 2 + x, 8 + a:24 + a, :] * up[0]
                s = s + m[c, x, 8 + a:24 + a, :] * dn[0]
                s = s + m[c, 1 + x, 9 + a:25 + a, :] * up[1]
                s = s + m[c, 1 + x, 7 + a:23 + a, :] * dn[1]
                s = s + rp * up[2]
                s = s + rm * dn[2]
                if low:
                    s = s * f
                    t = s * pv[c] if c == 0 else t + s * pv[c]
                o[c, x, a:a + 16, :] = s
            if low:
                tiles[pl.ds(x * na + a, 16), :] = t

    def stores(k):
        xs = pl.ds(k * XB, XB)
        return (
            pltpu.make_async_copy(olo.at[:, xs], upd.at[:, xs, :, 0:128], sem_out.at[k, 0]),
            pltpu.make_async_copy(ohi.at[:, xs], upd.at[:, xs, :, 128:256], sem_out.at[k, 1]),
        )

    for cp in halos:
        cp.wait()
    for cp in loads(0):
        cp.wait()
    lax.fori_loop(0, nx, edges, 0)
    mask(0)

    def block(k, _):
        @pl.when(k + 1 < nb)
        def _():
            for cp in loads(k + 1):
                cp.wait()

        def one(i, _):
            x = k * XB + i

            @pl.when(x + 1 < nx)
            def _():
                mask(x + 1)

            column(x, True)
            column(x, False)
            return 0

        lax.fori_loop(0, XB, one, 0)
        for cp in stores(k):
            cp.start()
        return 0

    lax.fori_loop(0, nb, block, 0)

    def scatter(i, _):
        for u in range(4):
            j = i * (4 * BANKS) + u * BANKS
            for b in range(BANKS):
                r = rows[j + b]
                banks[b][pl.ds(r, 1), :] = banks[b][pl.ds(r, 1), :] + tiles[pl.ds(j + b, 1), :]
        return 0

    lax.fori_loop(0, nx * na // (4 * BANKS), scatter, 0)

    n_half = keep.shape[0]

    def collect(i, _):
        lo = pl.ds(i * 32, 32)
        hi = pl.ds(n_half + i * 32, 32)
        keep[lo, :] = (bank0[lo, :] + bank1[lo, :]) + (bank2[lo, :] + bank3[lo, :])
        send[lo, :] = (bank0[hi, :] + bank1[hi, :]) + (bank2[hi, :] + bank3[hi, :])
        return 0

    lax.fori_loop(0, n_half // 32, collect, 0)

    def finish(k, _):
        for cp in stores(k):
            cp.wait()
        return 0

    lax.fori_loop(0, nb, finish, 0)


def grid_step(flags, rows, adjoint, primal, fluid, xp, xq, aa, ab, total_rows):
    _, nx, na, _ = adjoint.shape
    f32 = jnp.float32
    anyspace = pl.BlockSpec(memory_space=pl.ANY)
    vmem = pl.BlockSpec(memory_space=pltpu.VMEM)
    smem = pl.BlockSpec(memory_space=pltpu.SMEM)
    half_rows = total_rows // 2
    return pl.pallas_call(
        grid_kernel,
        out_shape=(
            jax.ShapeDtypeStruct(adjoint.shape, f32),
            jax.ShapeDtypeStruct((half_rows, 128), f32),
            jax.ShapeDtypeStruct((half_rows, 128), f32),
        ),
        in_specs=[smem, smem, anyspace, anyspace, vmem, anyspace, anyspace, vmem, vmem],
        out_specs=(anyspace, vmem, vmem),
        scratch_shapes=[
            pltpu.VMEM((3, nx + 2, na + 16, 128), f32),
            pltpu.VMEM((3, nx + 2, na + 16, 128), f32),
            pltpu.VMEM((3, nx, na, 128), f32),
            pltpu.VMEM((3, nx, na, 128), f32),
            pltpu.VMEM((3, nx, na, 128), f32),
            pltpu.VMEM((3, nx, na, 128), f32),
            pltpu.VMEM((nx * na, 128), f32),
        ] + [pltpu.VMEM((total_rows, 128), f32)] * BANKS + [
            pltpu.SemaphoreType.DMA((nx // XB, 4)),
            pltpu.SemaphoreType.DMA((2, 2)),
            pltpu.SemaphoreType.DMA((nx // XB, 2)),
        ],
        compiler_params=pltpu.CompilerParams(vmem_limit_bytes=60 << 20),
        name="grid_step",
    )(flags, rows, adjoint, primal, fluid, xp, xq, aa, ab)


def shards(adjoint, primal, wall, owner, adjacency, counts, laplacian):
    patches = laplacian.shape[1]
    vertices = laplacian.shape[2]
    neighbours_each = adjacency.shape[2]
    nx, na = wall.shape
    n_ax = lax.axis_size(AX)
    n_az = lax.axis_size(AZ)
    n_chip = lax.axis_size(CHIP)
    core = lax.axis_index("c")
    odd = lax.axis_index("z") % 2

    lane = lax.broadcasted_iota(jnp.int32, (nx, na, vertices), 2)
    fluid = (lane >= wall[:, :, None]).astype(jnp.float32)

    def masked(part, walls):
        depth = lax.broadcasted_iota(jnp.int32, part.shape[1:], part.ndim - 2)
        return jnp.where(depth >= walls[..., None], part, 0.0)

    a_first, a_last = masked(adjoint[:, :, 0], wall[:, 0]), masked(adjoint[:, :, na - 1], wall[:, na - 1])
    def halves(part):
        return jnp.stack([part[..., :128], part[..., 128:]])

    a_first, a_last = halves(a_first), halves(a_last)
    even_core = core == 0
    aa = lax.ppermute(jnp.where(even_core, a_last, a_first), AZ, pairs_a(n_az))
    ab = lax.ppermute(jnp.where(even_core, a_first, a_last), AZ, pairs_b(n_az))
    x_first, x_last = masked(adjoint[:, 0], wall[0]), masked(adjoint[:, nx - 1], wall[nx - 1])
    even_ax = odd == 0
    xp = lax.ppermute(jnp.where(even_ax, x_last, x_first), AX, pairs_a(n_ax))
    xq = lax.ppermute(jnp.where(even_ax, x_first, x_last), AX, pairs_q(n_ax))

    target = owner.reshape(-1) // patches
    within = owner.reshape(-1) % patches
    rows = ((target % 2) ^ core) * (n_chip * patches) + (target // 2) * patches + within
    flags = jnp.stack([core, odd]).astype(jnp.int32)

    updated, keep, send = grid_step(flags, rows, adjoint, primal, fluid, xp, xq, aa, ab, 2 * n_chip * patches)

    part = keep + lax.ppermute(send, "c", [(0, 1), (1, 0)])
    got = lax.all_to_all(part, CHIP, split_axis=0, concat_axis=0, tiled=True)
    source = jnp.sum(got.reshape(n_chip, patches, vertices), axis=0) * wall_scale

    vertex = lax.broadcasted_iota(jnp.int32, (patches, vertices), 1)
    live = (vertex < counts[0][:, None]).astype(jnp.float32)
    entry = adjacency[0]
    block = entry // patches
    place = jnp.where(even_core, block, 2 - block) * patches + entry % patches
    columns = jnp.arange(3 * patches, dtype=jnp.int32)
    incidence = jnp.sum((place[:, :, None] == columns[None, None, :]).astype(jnp.float32), axis=1)
    matrices = laplacian[0]
    field = live * source
    for sweep in range(SWEEPS):
        from_a = lax.ppermute(field, AZ, pairs_a(n_az))
        from_b = lax.ppermute(field, AZ, pairs_b(n_az))
        extended = jnp.concatenate([from_b, field, from_a], axis=0)
        neighbours = jnp.dot(incidence, extended, precision=lax.Precision.HIGHEST, preferred_element_type=jnp.float32)
        applied = jnp.einsum("pvw,pw->pv", matrices, field, precision=lax.Precision.HIGH)
        image = field + smoothing * (applied + coupling * (neighbours_each * field - neighbours))
        field = live * (field + relaxation * (source - image))
    return (updated, field[None])


def solution(mesh):
    fine = Mesh(np.asarray(mesh.devices).reshape(2, 4, 4, 2, 2), AX + AZ)
    in_specs = (
        P(None, AX, AZ, None),
        P(None, AX, AZ, None),
        P(AX, AZ),
        P(AX, AZ),
        P(AX, AZ, None),
        P(AX, AZ),
        P(AX, AZ, None, None),
    )
    out_specs = (P(None, AX, AZ, None), P(AX, AZ, None))
    return jax.shard_map(shards, mesh=fine, in_specs=in_specs, out_specs=out_specs, check_vma=False)
```

```python
import jax
import jax.numpy as jnp
import numpy as np
from jax import lax
from jax.experimental import pallas as pl
from jax.experimental.pallas import tpu as pltpu
from jax.sharding import Mesh, PartitionSpec as P

SWEEPS = 3
time_step = 0.12
viscosity = 1.0
wall_scale = 0.1
smoothing = 0.5
coupling = 0.25
relaxation = 0.25

CHIP = ("xh", "z", "y", "xl")
AX = ("xh", "z")
AZ = ("y", "xl", "c")
BANKS = 4
XB = 4


def pairs_a(n):
    return [(i, i ^ 1) for i in range(n)]


def pairs_b(n):
    return [(i, (i + 1) % n if i % 2 else (i - 1) % n) for i in range(n)]


def pairs_q(n):
    return [p for i in range(1, n - 1, 2) for p in ((i, i + 1), (i + 1, i))]


def load_all(pairs, sems, nb):
    def copies(k):
        out = []
        for n, (src, low, dst, pad) in enumerate(pairs):
            xs = pl.ds(k * XB, XB)
            if pad:
                d = dst.at[:, pl.ds(1 + k * XB, XB), 8:8 + src.shape[2], :]
            else:
                d = dst.at[:, xs]
            out.append(pltpu.make_async_copy(src.at[:, xs, :, low:low + 128], d, sems.at[k, n]))
        return out

    return copies


def to_column(row, eye):
    return jnp.sum(jnp.where(eye, row, 0.0), axis=1, keepdims=True)


def eye_mask(na):
    return lax.broadcasted_iota(jnp.int32, (na, na), 0) == lax.broadcasted_iota(jnp.int32, (na, na), 1)


def prep_kernel(adj, wall, owner, out_a, out_b, out_p, out_q, rows, buf0, buf1, bufx, sem):
    _, nx, na, _ = adj.shape
    core = lax.axis_index("c")
    odd = lax.rem(lax.axis_index("z"), 2)
    first = pltpu.make_async_copy(adj.at[:, :, 0:8, :], buf0, sem.at[0])
    last = pltpu.make_async_copy(adj.at[:, :, na - 8:na, :], buf1, sem.at[1])
    xi_p = jnp.where(odd == 0, nx - 1, 0)
    xi_q = jnp.where(odd == 0, 0, nx - 1)
    cps = [pltpu.make_async_copy(adj.at[:, i], bufx.at[n], sem.at[2 + n]) for n, i in enumerate((xi_p, xi_q))]
    first.start()
    last.start()
    for cp in cps:
        cp.start()
    own = owner[...]
    target = lax.shift_right_logical(own, 5)
    rows[...] = ((target & 1) ^ core) * 2048 + lax.shift_right_logical(target, 1) * 32 + (own & 31)
    lane_a = lax.broadcasted_iota(jnp.int32, (nx, 128), 1)
    w0 = lane_a >= wall[:, 0:1]
    w1 = lane_a >= wall[:, na - 1:na]
    first.wait()
    last.wait()
    even_core = core == 0
    for c in range(3):
        for h in range(2):
            f = buf0[c, :, 0, 128 * h:128 * h + 128]
            l = buf1[c, :, 7, 128 * h:128 * h + 128]
            if h == 0:
                f = jnp.where(w0, f, 0.0)
                l = jnp.where(w1, l, 0.0)
            out_a[h, c] = jnp.where(even_core, l, f)
            out_b[h, c] = jnp.where(even_core, f, l)
    eye = eye_mask(na)
    lane = lax.broadcasted_iota(jnp.int32, (na, 128), 1).astype(jnp.float32)
    for cp in cps:
        cp.wait()
    for n, (i, out) in enumerate(((xi_p, out_p), (xi_q, out_q))):
        keepers = lane >= to_column(wall[pl.ds(i, 1), :].astype(jnp.float32), eye)
        for c in range(3):
            out[0, c] = jnp.where(keepers, bufx[n, c, :, 0:128], 0.0)
            out[1, c] = bufx[n, c, :, 128:256]


def mid_kernel(rows, adj, prim, wall, aa, ab,
               upd, bank0, bank1, bank2, bank3, ecoef, eprim, eout,
               mlo, mhi, plo, olo, fluid, tiles, sem_in, sem_out):
    banks = (bank0, bank1, bank2, bank3)
    _, nx, na, _ = adj.shape
    nb = nx // XB
    core = lax.axis_index("c")
    loads = load_all(((adj, 0, mlo, True), (adj, 128, mhi, False), (prim, 0, plo, False)), sem_in, nb)

    def start(k, _):
        for cp in loads(k):
            cp.start()
        return 0

    lax.fori_loop(0, nb, start, 0)
    zero8 = jnp.zeros((64, 128), jnp.float32)

    def clear(i, _):
        for b in banks:
            b[pl.ds(i * 64, 64), :] = zero8
        return 0

    lax.fori_loop(0, bank0.shape[0] // 64, clear, 0)
    for c in range(3):
        mlo[c, 0, 8:8 + na, :] = jnp.zeros((na, 128), jnp.float32)
        mlo[c, nx + 1, 8:8 + na, :] = jnp.zeros((na, 128), jnp.float32)
    tiles[1] = jnp.zeros((na, 128), jnp.float32)

    row_a = jnp.where(core == 0, 8 + na, 7)
    row_b = jnp.where(core == 0, 7, 8 + na)

    def edges(x, _):
        for src, row in ((aa, row_a), (ab, row_b)):
            for c in range(3):
                mlo[c, 1 + x, pl.ds(row, 1), :] = src[0, c, pl.ds(x, 1), :]
        return 0

    lax.fori_loop(0, nx, edges, 0)

    eye = eye_mask(na)
    lane_f = lax.broadcasted_iota(jnp.int32, (na, 128), 1).astype(jnp.float32)

    def mask(x):
        f = (lane_f >= to_column(wall[pl.ds(x, 1), :].astype(jnp.float32), eye)).astype(jnp.float32)
        fluid[x] = f
        for c in range(3):
            mlo[c, 1 + x, 8:8 + na, :] = mlo[c, 1 + x, 8:8 + na, :] * f

    alpha = time_step * viscosity
    half = 0.5 * time_step
    lane = lax.broadcasted_iota(jnp.int32, (16, 128), 1)

    def spread(x, slot, a):
        for j in range(a, a + 16, BANKS):
            for b in range(BANKS):
                r = rows[x, j + b]
                banks[b][pl.ds(r, 1), :] = banks[b][pl.ds(r, 1), :] + tiles[slot, pl.ds(j + b, 1), :]

    def column(x, slot, before):
        for a in range(0, na, 16):
            pv = [plo[c, x, a:a + 16, :] for c in range(3)]
            q = [half * v for v in pv]
            up = [alpha + v for v in q]
            dn = [alpha - v for v in q]
            dn[2] = jnp.where(lane == 0, 0.0, dn[2])
            f = fluid[x, a:a + 16, :]
            t = None
            for c in range(3):
                mid = mlo[c, 1 + x, 8 + a:24 + a, :]
                oth = mhi[c, x, a:a + 16, :]
                rp = jnp.where(lane == 127, pltpu.roll(oth, 127, 1), pltpu.roll(mid, 127, 1))
                rm = pltpu.roll(mid, 1, 1)
                s = mid * (1.0 - 6.0 * alpha)
                s = s + mlo[c, 2 + x, 8 + a:24 + a, :] * up[0]
                s = s + mlo[c, x, 8 + a:24 + a, :] * dn[0]
                s = s + mlo[c, 1 + x, 9 + a:25 + a, :] * up[1]
                s = s + mlo[c, 1 + x, 7 + a:23 + a, :] * dn[1]
                s = s + rp * up[2]
                s = s + rm * dn[2]
                s = s * f
                t = s * pv[c] if c == 0 else t + s * pv[c]
                olo[c, x, a:a + 16, :] = s
            tiles[slot, a:a + 16, :] = t
            spread(before, 1 - slot, a)

    def stores(k):
        xs = pl.ds(k * XB, XB)
        return pltpu.make_async_copy(olo.at[:, xs], upd.at[:, xs, :, 0:128], sem_out.at[k])

    for cp in loads(0):
        cp.wait()
    mask(0)

    def block(k, _):
        @pl.when(k + 1 < nb)
        def _():
            for cp in loads(k + 1):
                cp.wait()

        def one(i, _):
            x = k * XB + 2 * i
            for u in range(2):
                mask(jnp.minimum(x + u + 1, nx - 1))
                column(x + u, u, jnp.maximum(x + u - 1, 0))
            return 0

        lax.fori_loop(0, XB // 2, one, 0)
        stores(k).start()
        return 0

    lax.fori_loop(0, nb, block, 0)
    for a in range(0, na, 16):
        spread(nx - 1, 1, a)
    for s, x in ((0, 0), (1, nx - 1)):
        q = half * plo[0, x]
        ecoef[s] = (alpha - q if s == 0 else alpha + q) * fluid[x]
        for c in range(3):
            eprim[c, s] = plo[c, x]
            eout[c, s] = olo[c, x]

    def finish(k, _):
        stores(k).wait()
        return 0

    lax.fori_loop(0, nb, finish, 0)


def edge_kernel(rows, xp, xq, ecoef, eprim, eout, b0, b1, b2, b3, upd_in,
                upd, keep, send, bank0, bank1, bank2, bank3, obuf, tiles, sem):
    banks = (bank0, bank1, bank2, bank3)
    _, nx, na, _ = upd.shape
    odd = lax.rem(lax.axis_index("z"), 2)
    even = odd == 0
    for s in range(2):
        t = None
        for c in range(3):
            a, b = (xq, xp) if s == 0 else (xp, xq)
            v = jnp.where(even, a[0, c], b[0, c]) * ecoef[s]
            obuf[c, s] = eout[c, s] + v
            t = eprim[c, s] * v if c == 0 else t + eprim[c, s] * v
        tiles[s] = t
    cps = [pltpu.make_async_copy(obuf.at[:, s], upd.at[:, x, :, 0:128], sem.at[s]) for s, x in ((0, 0), (1, nx - 1))]
    for cp in cps:
        cp.start()

    def spread(i, _):
        for s, x in ((0, 0), (1, nx - 1)):
            for b in range(BANKS):
                j = i * BANKS + b
                r = rows[x, j]
                banks[b][pl.ds(r, 1), :] = banks[b][pl.ds(r, 1), :] + tiles[s, pl.ds(j, 1), :]
        return 0

    lax.fori_loop(0, na // BANKS, spread, 0)
    n_half = keep.shape[0]

    def collect(i, _):
        lo = pl.ds(i * 32, 32)
        hi = pl.ds(n_half + i * 32, 32)
        keep[lo, :] = (bank0[lo, :] + bank1[lo, :]) + (bank2[lo, :] + bank3[lo, :])
        send[lo, :] = (bank0[hi, :] + bank1[hi, :]) + (bank2[hi, :] + bank3[hi, :])
        return 0

    lax.fori_loop(0, n_half // 32, collect, 0)
    for cp in cps:
        cp.wait()


def outer_kernel(adj, prim, aa, ab, xp, xq, upd_in, upd,
                 mhi, mlo, phi, ohi, sem_in, sem_out):
    _, nx, na, _ = adj.shape
    nb = nx // XB
    core = lax.axis_index("c")
    even = lax.rem(lax.axis_index("z"), 2) == 0
    loads = load_all(((adj, 128, mhi, True), (adj, 0, mlo, False), (prim, 128, phi, False)), sem_in, nb)

    def start(k, _):
        for cp in loads(k):
            cp.start()
        return 0

    lax.fori_loop(0, nb, start, 0)
    for c in range(3):
        mhi[c, 0, 8:8 + na, :] = jnp.where(even, xq[1, c], xp[1, c])
        mhi[c, nx + 1, 8:8 + na, :] = jnp.where(even, xp[1, c], xq[1, c])
    row_a = jnp.where(core == 0, 8 + na, 7)
    row_b = jnp.where(core == 0, 7, 8 + na)

    def edges(x, _):
        for src, row in ((aa, row_a), (ab, row_b)):
            for c in range(3):
                mhi[c, 1 + x, pl.ds(row, 1), :] = src[1, c, pl.ds(x, 1), :]
        return 0

    lax.fori_loop(0, nx, edges, 0)
    alpha = time_step * viscosity
    half = 0.5 * time_step
    lane = lax.broadcasted_iota(jnp.int32, (16, 128), 1)

    def column(x):
        for a in range(0, na, 16):
            q = [half * phi[c, x, a:a + 16, :] for c in range(3)]
            up = [alpha + v for v in q]
            dn = [alpha - v for v in q]
            up[2] = jnp.where(lane == 127, 0.0, up[2])
            for c in range(3):
                mid = mhi[c, 1 + x, 8 + a:24 + a, :]
                oth = mlo[c, x, a:a + 16, :]
                rp = pltpu.roll(mid, 127, 1)
                rm = jnp.where(lane == 0, pltpu.roll(oth, 1, 1), pltpu.roll(mid, 1, 1))
                s = mid * (1.0 - 6.0 * alpha)
                s = s + mhi[c, 2 + x, 8 + a:24 + a, :] * up[0]
                s = s + mhi[c, x, 8 + a:24 + a, :] * dn[0]
                s = s + mhi[c, 1 + x, 9 + a:25 + a, :] * up[1]
                s = s + mhi[c, 1 + x, 7 + a:23 + a, :] * dn[1]
                s = s + rp * up[2]
                s = s + rm * dn[2]
                ohi[c, x, a:a + 16, :] = s

    def stores(k):
        xs = pl.ds(k * XB, XB)
        return pltpu.make_async_copy(ohi.at[:, xs], upd.at[:, xs, :, 128:256], sem_out.at[k])

    for cp in loads(0):
        cp.wait()

    def block(k, _):
        @pl.when(k + 1 < nb)
        def _():
            for cp in loads(k + 1):
                cp.wait()

        def one(i, _):
            column(k * XB + i)
            return 0

        lax.fori_loop(0, XB, one, 0)
        stores(k).start()
        return 0

    lax.fori_loop(0, nb, block, 0)

    def finish(k, _):
        stores(k).wait()
        return 0

    lax.fori_loop(0, nb, finish, 0)


F32 = jnp.float32
ANYSPACE = pl.BlockSpec(memory_space=pl.ANY)
VMEM = pl.BlockSpec(memory_space=pltpu.VMEM)
SMEM = pl.BlockSpec(memory_space=pltpu.SMEM)


def shape(*dims, dtype=F32):
    return jax.ShapeDtypeStruct(dims, dtype)


def prep(adjoint, wall, owner):
    _, nx, na, nr = adjoint.shape
    return pl.pallas_call(
        prep_kernel,
        out_shape=(shape(2, 3, nx, 128), shape(2, 3, nx, 128), shape(2, 3, na, 128), shape(2, 3, na, 128),
                   shape(nx, na, dtype=jnp.int32)),
        in_specs=[ANYSPACE, VMEM, VMEM],
        out_specs=(VMEM,) * 5,
        scratch_shapes=[pltpu.VMEM((3, nx, 8, nr), F32), pltpu.VMEM((3, nx, 8, nr), F32),
                        pltpu.VMEM((2, 3, na, nr), F32), pltpu.SemaphoreType.DMA((4,))],
        compiler_params=pltpu.CompilerParams(vmem_limit_bytes=6 << 20),
        name="prep",
    )(adjoint, wall, owner)


def middle(rows, adjoint, primal, wall, aa, ab, total_rows):
    _, nx, na, _ = adjoint.shape
    nb = nx // XB
    return pl.pallas_call(
        mid_kernel,
        out_shape=(shape(*adjoint.shape),) + (shape(total_rows, 128),) * BANKS
        + (shape(2, na, 128), shape(3, 2, na, 128), shape(3, 2, na, 128)),
        in_specs=[SMEM, ANYSPACE, ANYSPACE, VMEM, VMEM, VMEM],
        out_specs=(ANYSPACE,) + (VMEM,) * (BANKS + 3),
        scratch_shapes=[
            pltpu.VMEM((3, nx + 2, na + 16, 128), F32),
            pltpu.VMEM((3, nx, na, 128), F32),
            pltpu.VMEM((3, nx, na, 128), F32),
            pltpu.VMEM((3, nx, na, 128), F32),
            pltpu.VMEM((nx, na, 128), F32),
            pltpu.VMEM((2, na, 128), F32),
            pltpu.SemaphoreType.DMA((nb, 3)),
            pltpu.SemaphoreType.DMA((nb,)),
        ],
        compiler_params=pltpu.CompilerParams(vmem_limit_bytes=27 << 20),
        name="middle",
    )(rows, adjoint, primal, wall, aa, ab)


def edge(rows, xp, xq, ecoef, eprim, eout, banks, upd):
    _, nx, na, _ = upd.shape
    half_rows = banks[0].shape[0] // 2
    out = pl.pallas_call(
        edge_kernel,
        out_shape=(shape(*upd.shape), shape(half_rows, 128), shape(half_rows, 128))
        + tuple(shape(*b.shape) for b in banks),
        in_specs=[SMEM] + [VMEM] * (5 + BANKS) + [ANYSPACE],
        out_specs=(ANYSPACE,) + (VMEM,) * (2 + BANKS),
        input_output_aliases={6 + BANKS: 0, 6: 3, 7: 4, 8: 5, 9: 6},
        scratch_shapes=[pltpu.VMEM((3, 2, na, 128), F32), pltpu.VMEM((2, na, 128), F32), pltpu.SemaphoreType.DMA((2,))],
        compiler_params=pltpu.CompilerParams(vmem_limit_bytes=14 << 20),
        name="edge",
    )(rows, xp, xq, ecoef, eprim, eout, *banks, upd)
    return out[0], out[1], out[2]


def outer(adjoint, primal, aa, ab, xp, xq, upd):
    _, nx, na, _ = adjoint.shape
    nb = nx // XB
    return pl.pallas_call(
        outer_kernel,
        out_shape=shape(*adjoint.shape),
        in_specs=[ANYSPACE, ANYSPACE, VMEM, VMEM, VMEM, VMEM, ANYSPACE],
        out_specs=ANYSPACE,
        input_output_aliases={6: 0},
        scratch_shapes=[
            pltpu.VMEM((3, nx + 2, na + 16, 128), F32),
            pltpu.VMEM((3, nx, na, 128), F32),
            pltpu.VMEM((3, nx, na, 128), F32),
            pltpu.VMEM((3, nx, na, 128), F32),
            pltpu.SemaphoreType.DMA((nb, 3)),
            pltpu.SemaphoreType.DMA((nb,)),
        ],
        compiler_params=pltpu.CompilerParams(vmem_limit_bytes=16 << 20),
        name="outer",
    )(adjoint, primal, aa, ab, xp, xq, upd)


def shards(adjoint, primal, wall, owner, adjacency, counts, laplacian):
    patches = laplacian.shape[1]
    vertices = laplacian.shape[2]
    neighbours_each = adjacency.shape[2]
    nx, na = wall.shape
    n_ax = lax.axis_size(AX)
    n_az = lax.axis_size(AZ)
    n_chip = lax.axis_size(CHIP)
    core = lax.axis_index("c")
    even_core = core == 0
    pay_a, pay_b, pay_p, pay_q, rows = prep(adjoint, wall, owner)
    aa = lax.ppermute(pay_a, AZ, pairs_a(n_az))
    ab = lax.ppermute(pay_b, AZ, pairs_b(n_az))
    xp = lax.ppermute(pay_p, AX, pairs_a(n_ax))
    xq = lax.ppermute(pay_q, AX, pairs_q(n_ax))
    upd, *rest = middle(rows, adjoint, primal, wall, aa, ab, 2 * n_chip * patches)
    banks, (ecoef, eprim, eout) = rest[:BANKS], rest[BANKS:]
    upd, keep, send = edge(rows, xp, xq, ecoef, eprim, eout, banks, upd)
    updated = outer(adjoint, primal, aa, ab, xp, xq, upd)

    part = keep + lax.ppermute(send, "c", [(0, 1), (1, 0)])
    got = lax.all_to_all(part, CHIP, split_axis=0, concat_axis=0, tiled=True)
    source = jnp.sum(got.reshape(n_chip, patches, vertices), axis=0) * wall_scale

    vertex = lax.broadcasted_iota(jnp.int32, (patches, vertices), 1)
    live = (vertex < counts[0][:, None]).astype(jnp.float32)
    entry = adjacency[0]
    block = entry // patches
    place = jnp.where(even_core, block, 2 - block) * patches + entry % patches
    columns = jnp.arange(3 * patches, dtype=jnp.int32)
    incidence = jnp.sum((place[:, :, None] == columns[None, None, :]).astype(jnp.float32), axis=1)
    matrices = laplacian[0]
    field = live * source
    for sweep in range(SWEEPS):
        from_a = lax.ppermute(field, AZ, pairs_a(n_az))
        from_b = lax.ppermute(field, AZ, pairs_b(n_az))
        extended = jnp.concatenate([from_b, field, from_a], axis=0)
        neighbours = jnp.dot(incidence, extended, precision=lax.Precision.HIGHEST, preferred_element_type=jnp.float32)
        applied = jnp.einsum("pvw,pw->pv", matrices, field, precision=lax.Precision.HIGH)
        image = field + smoothing * (applied + coupling * (neighbours_each * field - neighbours))
        field = live * (field + relaxation * (source - image))
    return (updated, field[None])


def solution(mesh):
    fine = Mesh(np.asarray(mesh.devices).reshape(2, 4, 4, 2, 2), AX + AZ)
    in_specs = (
        P(None, AX, AZ, None),
        P(None, AX, AZ, None),
        P(AX, AZ),
        P(AX, AZ),
        P(AX, AZ, None),
        P(AX, AZ),
        P(AX, AZ, None, None),
    )
    out_specs = (P(None, AX, AZ, None), P(AX, AZ, None))
    return jax.shard_map(shards, mesh=fine, in_specs=in_specs, out_specs=out_specs, check_vma=False)
```
